128 devices in a mesh: fsdp: 64 (over z, x_hi, y, core), tensor: 2 (over x_lo).
Axes of the slice: x: 4 (x_hi: 2, x_lo: 2; x = x_hi * 2 + x_lo), y: 4, z: 4, core: 2. Of those that a mesh axis runs over, the one named last changes fastest.
Arguments:
- tokens: bfloat16 [8192, 1024], P('fsdp'), may hold values from -6 to 6
- segment: int32 [8192], P('fsdp'), may hold values from 0 to 8191, as said below
- w_query: bfloat16 [1024, 1024], P('fsdp', 'tensor'), may hold values from -0.1875 to 0.1875
- w_key: bfloat16 [1024, 512], P('fsdp', 'tensor'), may hold values from -0.1875 to 0.1875
- w_value: bfloat16 [1024, 512], P('fsdp', 'tensor'), may hold values from -0.1875 to 0.1875
- w_output: bfloat16 [1024, 1024], P('tensor', 'fsdp'), may hold values from -0.5 to 0.5
- w_gate: bfloat16 [1024, 4608], P('fsdp', 'tensor'), may hold values from -0.1875 to 0.1875
- w_up: bfloat16 [1024, 4608], P('fsdp', 'tensor'), may hold values from -0.1875 to 0.1875
- w_down: bfloat16 [4608, 1024], P('tensor', 'fsdp'), may hold values from -0.09375 to 0.09375
- norm_attn: bfloat16 [1024], P('fsdp'), may hold values from 0.25 to 1.75
- norm_ffn: bfloat16 [1024], P('fsdp'), may hold values from 0.25 to 1.75
- norm_query: bfloat16 [64], P('fsdp'), may hold values from 0.25 to 1.75
- norm_key: bfloat16 [64], P('fsdp'), may hold values from 0.25 to 1.75
- cotangent: bfloat16 [8192, 1024], P('fsdp'), may hold values from -16 to 16
Outputs:
- block_out: bfloat16 [8192, 1024], P('fsdp')
- grad_tokens: bfloat16 [8192, 1024], P('fsdp')
- grad_query: float32 [1024, 1024], P('fsdp', 'tensor')
- grad_key: float32 [1024, 512], P('fsdp', 'tensor')
- grad_value: float32 [1024, 512], P('fsdp', 'tensor')
- grad_output: float32 [1024, 1024], P('tensor', 'fsdp')
- grad_gate: float32 [1024, 4608], P('fsdp', 'tensor')
- grad_up: float32 [1024, 4608], P('fsdp', 'tensor')
- grad_down: float32 [4608, 1024], P('tensor', 'fsdp')
- grad_norm_attn: float32 [1024], P('fsdp')
- grad_norm_ffn: float32 [1024], P('fsdp')
- grad_norm_query: float32 [64], P('fsdp')
- grad_norm_key: float32 [64], P('fsdp')
The draws below stay inside these ranges and needn't reach their ends.
Inputs may be any that keep to these rules, and one draw needn't show every extreme that they name: `segment`: ids never fall; all tokens of an id lie in one aligned block of 128 tokens; the first and the last token of every such block start a new id.
All inputs are finite; a program needn't handle non-finite values.
Results may differ from the reference program's by a relative error of at most 0.019.
Values may be sent and summed in bfloat16 or wider, within the bound.
No kernel may reach another device: no remote copies, remote signals or barrier semaphores. Data moves between devices by JAX's collectives and lax.ppermute only.
A program may use at most 128 MiB of HBM per device.

```python
import jax
import jax.numpy as jnp
from jax import lax

D = 1024
H = 16
KV = 8
HD = 64
FF = 4608
TOK_DEV = 128
TOKENS = 8192


def draw_segment(key, part):
    first_key, second_key = jax.random.split(jax.random.fold_in(key, 11))
    blocks = TOKENS // TOK_DEV
    spacing = jax.random.randint(first_key, (blocks, 1), 2, TOK_DEV // 2 + 1)
    coin_draw = jax.random.randint(second_key, (blocks, TOK_DEV), 0, 1 << 20)
    column = jnp.arange(TOK_DEV, dtype=jnp.int32)[None, :]
    starts = (coin_draw % spacing == 0) | (column == 0) | (column == TOK_DEV - 1)
    index_all = jnp.arange(TOKENS, dtype=jnp.int32)
    marked = jnp.where(starts.reshape(-1), index_all, jnp.zeros_like(index_all))
    return lax.cummax(marked, axis=0).astype(jnp.int32)


def strengthened(entries, rng, source, target, parts, factor):
    def block_of(axis_at):
        return (jnp.arange(entries.shape[axis_at]) // (entries.shape[axis_at] // parts)).reshape((-1,) + (1,) * (entries.ndim - 1 - axis_at))

    one_side = jax.random.permutation(rng, parts)[block_of(target)]
    second = (block_of(target) + parts // 2) % parts
    return jnp.where((block_of(source) == one_side) | (block_of(source) == second), factor * entries, entries)


def steps_of(own_key, shape, cuts, smallest, largest):
    level = 1.0
    for axis_at, shards_of in cuts:
        heights = jax.random.uniform(jax.random.fold_in(jax.random.fold_in(own_key, 6), axis_at), (shards_of,), jnp.float32, smallest / len(cuts), largest / len(cuts))
        level = level * jnp.repeat(jnp.exp(heights), shape[axis_at] // shards_of).reshape((-1,) + (1,) * (len(shape) - 1 - axis_at))
    return level


def gaussian(rng, dims, width, bound, pieces=(), held_as=jnp.bfloat16):
    drawn = jax.random.normal(rng, dims, jnp.float32) * width
    if len(pieces) > 0:
        drawn = steps_of(rng, dims, pieces, -0.22, 0.18) * drawn
    return jnp.clip(drawn, min=-bound, max=bound).astype(held_as)


def heavy_noise(own_key, extent, scale, bound, cuts, heavy, kind=jnp.bfloat16):
    array = scale * jax.random.normal(own_key, extent, jnp.float32)
    if cuts:
        array = array * steps_of(own_key, extent, cuts, -0.22, 0.18)
    return jnp.clip(strengthened(array, jax.random.fold_in(own_key, 3), *heavy), -bound, bound).astype(kind)


def setup_inputs(seed: int = 0) -> dict:
    seeds = jax.random.split(jax.random.key(seed), 15)
    return {
        "tokens": gaussian(seeds[0], (TOKENS, D), 1.0, 6.0, ((0, 64),)),
        "segment": draw_segment(jax.random.fold_in(seeds[14], 71), 0),
        "w_query": gaussian(seeds[2], (D, H * HD), D ** -0.5, 0.1875, ((0, 64), (1, 2))),
        "w_key": gaussian(seeds[3], (D, KV * HD), D ** -0.5, 0.1875, ((0, 64), (1, 2))),
        "w_value": gaussian(seeds[4], (D, KV * HD), D ** -0.5, 0.1875, ((0, 64), (1, 2))),
        "w_output": gaussian(seeds[5], (H * HD, D), (2 * HD) ** -0.5, 0.5, ((0, 2), (1, 64))),
        "w_gate": gaussian(seeds[6], (D, FF), D ** -0.5, 0.1875, ((0, 64), (1, 2))),
        "w_up": gaussian(seeds[7], (D, FF), D ** -0.5, 0.1875, ((0, 64), (1, 2))),
        "w_down": gaussian(seeds[8], (FF, D), FF ** -0.5, 0.09375, ((0, 2), (1, 64))),
        "norm_attn": jnp.clip(1.0 + 0.15 * jax.random.normal(seeds[9], (D,), jnp.float32), 0.25, 1.75).astype(jnp.bfloat16),
        "norm_ffn": jnp.clip(1.0 + 0.15 * jax.random.normal(seeds[10], (D,), jnp.float32), 0.25, 1.75).astype(jnp.bfloat16),
        "norm_query": jnp.clip(1.0 + 0.15 * jax.random.normal(seeds[11], (HD,), jnp.float32), 0.25, 1.75).astype(jnp.bfloat16),
        "norm_key": jnp.clip(1.0 + 0.15 * jax.random.normal(seeds[12], (HD,), jnp.float32), 0.25, 1.75).astype(jnp.bfloat16),
        "cotangent": heavy_noise(seeds[13], (TOKENS, D), 1.0, 16.0, ((0, 64),), (0, 1, 64, 4.0)),
    }


epsilon = 1e-05
rope_base = 1000000.0

def matmul(matrix, second):
    return jnp.dot(matrix, second, preferred_element_type=jnp.float32)

def contract(pattern, matrix, second):
    return jnp.einsum(pattern, matrix.astype(jnp.float32), second.astype(jnp.float32))

def normalize(vector):
    inverse = lax.rsqrt(lax.optimization_barrier(jnp.mean(vector * vector, axis=-1, keepdims=True)) + epsilon)
    return (vector * inverse, inverse)

def norm_back(grad_in, normed, inverse):
    return inverse * (grad_in - normed * lax.optimization_barrier(jnp.mean(grad_in * normed, axis=-1, keepdims=True)))

def rotate(vector):
    half_size = vector.shape[-1] // 2
    return jnp.concatenate([-vector[..., half_size:], vector[..., :half_size]], axis=-1)

def rotate_back(vector):
    half_size = vector.shape[-1] // 2
    return jnp.concatenate([vector[..., half_size:], -vector[..., :half_size]], axis=-1)

def tables(segment, head_size):
    row_count = segment.shape[0]
    row_index = jnp.arange(row_count, dtype=jnp.int32)
    same_segment = segment[:, None] == segment[None, :]
    first_row = lax.optimization_barrier(jnp.min(jnp.where(same_segment, row_index[None, :], row_count), axis=1))
    position = (row_index - first_row).astype(jnp.float32)
    allowed = same_segment & (row_index[None, :] <= row_index[:, None])
    half_size = head_size // 2
    frequency = jnp.power(rope_base, -2.0 * jnp.arange(half_size, dtype=jnp.float32) / head_size)
    phase_angle = position[:, None] * frequency[None, :]
    phase_angle = jnp.concatenate([phase_angle, phase_angle], axis=1)
    return (allowed, jnp.cos(phase_angle)[:, None, :], jnp.sin(phase_angle)[:, None, :])

def head_prep(raw_heads, head_gain, cos_table, sin_table):
    unit_heads, inverse = normalize(raw_heads)
    scaled = unit_heads * head_gain
    return (scaled * cos_table + rotate(scaled) * sin_table, unit_heads, inverse)

def head_back(grad_in, unit_heads, inverse, head_gain, cos_table, sin_table):
    grad_scaled = grad_in * cos_table + rotate_back(grad_in * sin_table)
    gain_grad = lax.optimization_barrier(jnp.sum(grad_scaled * unit_heads, axis=(0, 1)))
    return (norm_back(grad_scaled * head_gain, unit_heads, inverse), gain_grad)

def score_block(query_heads, key_heads, allowed):
    row_count, head_count, head_size = query_heads.shape
    kv_count = key_heads.shape[1]
    query_groups = query_heads.reshape(row_count, kv_count, head_count // kv_count, head_size)
    scores = contract('ikgd,jkd->kgij', query_groups, key_heads) * head_size ** (-0.5)
    return (query_groups, jnp.where(allowed, scores, -1e+30))

def attend(query_heads, key_heads, value_heads, allowed):
    row_count, head_count, head_size = query_heads.shape
    query_groups, masked = score_block(query_heads, key_heads, allowed)
    row_max = lax.optimization_barrier(jnp.max(masked, axis=-1, keepdims=True))
    exp_scores = jnp.exp(masked - row_max)
    denominator = lax.optimization_barrier(jnp.sum(exp_scores, axis=-1, keepdims=True))
    log_total = row_max + jnp.log(denominator)
    attn_weights = (exp_scores / denominator).astype(jnp.bfloat16)
    mixed = contract('kgij,jkd->ikgd', attn_weights, value_heads).astype(jnp.bfloat16)
    return (mixed.reshape(row_count, head_count * head_size), log_total)

def attend_back(query_heads, key_heads, value_heads, attended, grad_attended, log_total, allowed):
    row_count, head_count, head_size = query_heads.shape
    kv_count = key_heads.shape[1]
    group_size = head_count // kv_count
    query_groups, masked = score_block(query_heads, key_heads, allowed)
    prob = jnp.exp(masked - log_total)
    prob_low = prob.astype(jnp.bfloat16)
    grad_groups = grad_attended.reshape(row_count, kv_count, group_size, head_size)
    out_groups = attended.reshape(row_count, kv_count, group_size, head_size)
    row_delta = lax.optimization_barrier(jnp.sum(grad_groups.astype(jnp.float32) * out_groups.astype(jnp.float32), axis=-1))
    row_delta = jnp.transpose(row_delta, (1, 2, 0))[..., None]
    grad_kv_value = contract('kgij,ikgd->jkd', prob_low, grad_groups)
    grad_prob = contract('ikgd,jkd->kgij', grad_groups, value_heads)
    grad_scores = (prob * (grad_prob - row_delta) * head_size ** (-0.5)).astype(jnp.bfloat16)
    grad_query = contract('kgij,jkd->ikgd', grad_scores, key_heads).reshape(row_count, head_count, head_size)
    grad_key = contract('kgij,ikgd->jkd', grad_scores, query_groups)
    return (grad_query, grad_key, grad_kv_value)

def block(tokens, segment, cotangent, weights):
    w_query, w_key, w_value, w_output, w_gate, w_up, w_down, norm_attn, norm_ffn, norm_query, norm_key = weights
    row_count = tokens.shape[0]
    head_size = norm_query.shape[0]
    head_count = w_query.shape[1] // head_size
    kv_count = w_key.shape[1] // head_size
    allowed, cos_table, sin_table = tables(segment, head_size)
    inputs = tokens.astype(jnp.float32)
    normed_one, inv_one = normalize(inputs)
    hidden_one = (normed_one * norm_attn).astype(jnp.bfloat16)
    query_raw = matmul(hidden_one, w_query).reshape(row_count, head_count, head_size)
    key_raw = matmul(hidden_one, w_key).reshape(row_count, kv_count, head_size)
    value_heads = matmul(hidden_one, w_value).astype(jnp.bfloat16).reshape(row_count, kv_count, head_size)
    query_rot, query_unit, query_inv = head_prep(query_raw, norm_query, cos_table, sin_table)
    key_rot, key_unit, key_inv = head_prep(key_raw, norm_key, cos_table, sin_table)
    query_heads = query_rot.astype(jnp.bfloat16)
    key_heads = key_rot.astype(jnp.bfloat16)
    attended, log_total = attend(query_heads, key_heads, value_heads, allowed)
    residual = inputs + matmul(attended, w_output)
    normed_two, inv_two = normalize(residual)
    hidden_two = (normed_two * norm_ffn).astype(jnp.bfloat16)
    gate_pre = matmul(hidden_two, w_gate)
    up_pre = matmul(hidden_two, w_up)
    sigmoid_gate = jax.nn.sigmoid(gate_pre)
    activation = (gate_pre * sigmoid_gate * up_pre).astype(jnp.bfloat16)
    block_out = (residual + matmul(activation, w_down)).astype(jnp.bfloat16)
    grad_down = matmul(activation.T, cotangent)
    grad_act = matmul(cotangent, w_down.T)
    grad_gate_pre = (grad_act * up_pre * sigmoid_gate * (1.0 + gate_pre * (1.0 - sigmoid_gate))).astype(jnp.bfloat16)
    grad_up_pre = (grad_act * gate_pre * sigmoid_gate).astype(jnp.bfloat16)
    grad_gate = matmul(hidden_two.T, grad_gate_pre)
    grad_up = matmul(hidden_two.T, grad_up_pre)
    grad_hidden_two = matmul(grad_gate_pre, w_gate.T) + matmul(grad_up_pre, w_up.T)
    grad_norm_ffn = lax.optimization_barrier(jnp.sum(grad_hidden_two * normed_two, axis=0))
    grad_residual = cotangent.astype(jnp.float32) + norm_back(grad_hidden_two * norm_ffn, normed_two, inv_two)
    grad_res_low = grad_residual.astype(jnp.bfloat16)
    grad_output = matmul(attended.T, grad_res_low)
    grad_attended = matmul(grad_res_low, w_output.T).astype(jnp.bfloat16)
    grad_q_rot, grad_k_rot, grad_kv_value = attend_back(query_heads, key_heads, value_heads, attended, grad_attended, log_total, allowed)
    grad_q_raw, grad_norm_query = head_back(grad_q_rot, query_unit, query_inv, norm_query, cos_table, sin_table)
    grad_k_raw, grad_norm_key = head_back(grad_k_rot, key_unit, key_inv, norm_key, cos_table, sin_table)
    query_low = grad_q_raw.reshape(row_count, head_count * head_size).astype(jnp.bfloat16)
    key_low = grad_k_raw.reshape(row_count, kv_count * head_size).astype(jnp.bfloat16)
    value_low = grad_kv_value.reshape(row_count, kv_count * head_size).astype(jnp.bfloat16)
    grad_query = matmul(hidden_one.T, query_low)
    grad_key = matmul(hidden_one.T, key_low)
    grad_value = matmul(hidden_one.T, value_low)
    grad_hidden_one = matmul(query_low, w_query.T) + matmul(key_low, w_key.T) + matmul(value_low, w_value.T)
    grad_norm_attn = lax.optimization_barrier(jnp.sum(grad_hidden_one * normed_one, axis=0))
    grad_tokens = (grad_residual + norm_back(grad_hidden_one * norm_attn, normed_one, inv_one)).astype(jnp.bfloat16)
    grad_list = (grad_query, grad_key, grad_value, grad_output, grad_gate, grad_up, grad_down, grad_norm_attn, grad_norm_ffn, grad_norm_query, grad_norm_key)
    return (block_out, grad_tokens, grad_list)

def reference(tokens, segment, w_query, w_key, w_value, w_output, w_gate, w_up, w_down, norm_attn, norm_ffn, norm_query, norm_key, cotangent):
    weights = (w_query, w_key, w_value, w_output, w_gate, w_up, w_down, norm_attn, norm_ffn, norm_query, norm_key)
    blocks = TOKENS // TOK_DEV
    token_blocks = tokens.reshape(blocks, TOK_DEV, D)
    segment_blocks = segment.reshape(blocks, TOK_DEV)
    cot_blocks = cotangent.reshape(blocks, TOK_DEV, D)
    start_sums = tuple((jnp.zeros(weight.shape, jnp.float32) for weight in weights))

    def scan_step(running, block_piece):
        token_part, segment_part, cot_part = block_piece
        out_part, grad_part, grad_list = block(token_part, segment_part, cot_part, weights)
        return (tuple((acc + new for acc, new in zip(running, grad_list))), (out_part, grad_part))
    sums, (outs_all, grads_all) = lax.scan(scan_step, start_sums, (token_blocks, segment_blocks, cot_blocks))
    return (outs_all.reshape(TOKENS, D), grads_all.reshape(TOKENS, D), sums[0], sums[1], sums[2], sums[3], sums[4], sums[5], sums[6], sums[7], sums[8], sums[9], sums[10])
```

```python
import jax
import jax.numpy as jnp
from jax import lax
from jax.sharding import Mesh
from jax.sharding import PartitionSpec as P

epsilon = 1e-05
rope_base = 1000000.0
bf16 = jnp.bfloat16
f32 = jnp.float32
FSDP = ("z", "h", "y", "c")
BITS = {
    "c": ("c", 2, 1),
    "ya": ("y", 4, 1),
    "yb": ("y", 4, 3),
    "za": ("z", 4, 1),
    "zb": ("z", 4, 3),
    "h": ("h", 2, 1),
}


def matmul(matrix, second):
    return jnp.dot(matrix, second, preferred_element_type=f32)


def matmul_tr(matrix, second):
    return lax.dot_general(matrix, second, (((1,), (1,)), ((), ())), preferred_element_type=f32)


def tr_matmul(matrix, second):
    return lax.dot_general(matrix, second, (((0,), (0,)), ((), ())), preferred_element_type=f32)


def contract(pattern, matrix, second):
    return jnp.einsum(pattern, matrix, second, preferred_element_type=f32)


def normalize(vector):
    inverse = lax.rsqrt(jnp.mean(vector * vector, axis=-1, keepdims=True) + epsilon)
    return (vector * inverse, inverse)


def norm_back(grad_in, normed, inverse):
    return inverse * (grad_in - normed * jnp.mean(grad_in * normed, axis=-1, keepdims=True))


def rotate(vector):
    half_size = vector.shape[-1] // 2
    return jnp.concatenate([-vector[..., half_size:], vector[..., :half_size]], axis=-1)


def rotate_back(vector):
    half_size = vector.shape[-1] // 2
    return jnp.concatenate([vector[..., half_size:], -vector[..., :half_size]], axis=-1)


def tables(segment, head_size):
    row_count = segment.shape[0]
    row_index = jnp.arange(row_count, dtype=jnp.int32)
    same_segment = segment[:, None] == segment[None, :]
    first_row = jnp.min(jnp.where(same_segment, row_index[None, :], row_count), axis=1)
    position = (row_index - first_row).astype(f32)
    allowed = same_segment & (row_index[None, :] <= row_index[:, None])
    half_size = head_size // 2
    frequency = jnp.power(rope_base, -2.0 * jnp.arange(half_size, dtype=f32) / head_size)
    phase_angle = position[:, None] * frequency[None, :]
    phase_angle = jnp.concatenate([phase_angle, phase_angle], axis=1)
    return (allowed, jnp.cos(phase_angle)[:, None, :], jnp.sin(phase_angle)[:, None, :])


def head_prep(raw_heads, head_gain, cos_table, sin_table):
    unit_heads, inverse = normalize(raw_heads)
    scaled = unit_heads * head_gain
    return (scaled * cos_table + rotate(scaled) * sin_table, unit_heads, inverse)


def head_back(grad_in, unit_heads, inverse, head_gain, cos_table, sin_table):
    grad_scaled = grad_in * cos_table + rotate_back(grad_in * sin_table)
    gain_grad = jnp.sum(grad_scaled * unit_heads, axis=(0, 1))
    return (norm_back(grad_scaled * head_gain, unit_heads, inverse), gain_grad)


def score_block(query_heads, key_heads, allowed):
    row_count, head_count, head_size = query_heads.shape
    kv_count = key_heads.shape[1]
    query_groups = query_heads.reshape(row_count, kv_count, head_count // kv_count, head_size)
    scores = contract("ikgd,jkd->kgij", query_groups, key_heads) * head_size ** (-0.5)
    return (query_groups, jnp.where(allowed, scores, -1e30))


def attend(query_heads, key_heads, value_heads, allowed):
    row_count, head_count, head_size = query_heads.shape
    query_groups, masked = score_block(query_heads, key_heads, allowed)
    row_max = jnp.max(masked, axis=-1, keepdims=True)
    exp_scores = jnp.exp(masked - row_max)
    denominator = jnp.sum(exp_scores, axis=-1, keepdims=True)
    log_total = row_max + jnp.log(denominator)
    attn_weights = (exp_scores / denominator).astype(bf16)
    mixed = contract("kgij,jkd->ikgd", attn_weights, value_heads).astype(bf16)
    return (mixed.reshape(row_count, head_count * head_size), log_total)


def attend_back(query_heads, key_heads, value_heads, attended, grad_attended, log_total, allowed):
    row_count, head_count, head_size = query_heads.shape
    kv_count = key_heads.shape[1]
    group_size = head_count // kv_count
    query_groups, masked = score_block(query_heads, key_heads, allowed)
    prob = jnp.exp(masked - log_total)
    prob_low = prob.astype(bf16)
    grad_groups = grad_attended.reshape(row_count, kv_count, group_size, head_size)
    out_groups = attended.reshape(row_count, kv_count, group_size, head_size)
    row_delta = jnp.sum(grad_groups.astype(f32) * out_groups.astype(f32), axis=-1)
    row_delta = jnp.transpose(row_delta, (1, 2, 0))[..., None]
    grad_kv_value = contract("kgij,ikgd->jkd", prob_low, grad_groups)
    grad_prob = contract("ikgd,jkd->kgij", grad_groups, value_heads)
    grad_scores = (prob * (grad_prob - row_delta) * head_size ** (-0.5)).astype(bf16)
    grad_query = contract("kgij,jkd->ikgd", grad_scores, key_heads).reshape(
        row_count, head_count, head_size
    )
    grad_key = contract("kgij,ikgd->jkd", grad_scores, query_groups)
    return (grad_query, grad_key, grad_kv_value)


def swap(array, bit):
    axis, size, flip = BITS[bit]
    return lax.ppermute(array, axis, [(i, i ^ flip) for i in range(size)])


def swap_pair(low):
    return lax.ppermute(low, "t", [(0, 1), (1, 0)])


def add_pair(low, other):
    return low.astype(f32) + other.astype(f32)


def absolute_rows(width):
    block = width // 64
    r = lax.broadcasted_iota(jnp.int32, (1, width), 1)
    k = r % block
    bits = r // block
    h, zb, za, yb, ya, c = ((bits >> i) & 1 for i in range(6))
    z_at = lax.axis_index("z") ^ za ^ (3 * zb)
    y_at = lax.axis_index("y") ^ ya ^ (3 * yb)
    h_at = lax.axis_index("h") ^ h
    c_at = lax.axis_index("c") ^ c
    return (((z_at * 2 + h_at) * 4 + y_at) * 2 + c_at) * block + k


ORDERS = (
    ("ya", "yb", "za", "zb", "h"),
    ("yb", "ya", "zb", "za", "h"),
    ("za", "zb", "ya", "yb", "h"),
    ("zb", "za", "yb", "ya", "h"),
)
INNER = ("ya", "yb", "za", "zb", "h")


def exchange(arrays, bits, after=()):
    arrays = lax.optimization_barrier(tuple(arrays) + tuple(after))[: len(arrays)]
    return [swap(a.reshape(-1, a.shape[-1]), b).reshape(a.shape) for a, b in zip(arrays, bits)]


def join(first, second):
    both = lax.optimization_barrier(tuple(first) + tuple(second))
    return list(both[: len(first)]), list(both[len(first) :])


class Gather:
    def __init__(self, pack, order):
        self.held = pack
        self.order = order[::-1]
        self.names = []

    def take(self, got):
        bit = self.order[len(self.names)]
        self.names = [n for n in INNER if n in self.names or n == bit]
        self.held = jnp.stack([self.held, got], axis=self.names.index(bit))

    @property
    def bit(self):
        return self.order[len(self.names)]

    def rows(self):
        return self.held.reshape(-1, self.held.shape[-1])


class Reduce:
    def __init__(self, order):
        self.order = order
        self.names = list(INNER)

    def begin(self, own, got):
        held = (own + got.astype(f32)).astype(bf16)
        rows = held.shape[0] // 2 ** len(self.names)
        self.held = held.reshape((2,) * len(self.names) + (rows, held.shape[1]))

    @property
    def bit(self):
        return self.order[len(INNER) - len(self.names)]

    def give(self):
        return lax.index_in_dim(self.held, 1, self.names.index(self.bit), keepdims=False)

    def take(self, got):
        own = lax.index_in_dim(self.held, 0, self.names.index(self.bit), keepdims=False)
        self.names.remove(self.bit)
        self.held = own.astype(f32) + got.astype(f32)
        if self.names:
            self.held = self.held.astype(bf16)


def advance(streams, after=()):
    gots = exchange([s.give() for s in streams], [s.bit for s in streams], after)
    for stream, got in zip(streams, gots):
        stream.take(got)


def tie(streams, values):
    held, values = join([s.held for s in streams], values)
    for stream, array in zip(streams, held):
        stream.held = array
    return values


def on_device(
    tokens,
    segment,
    w_query,
    w_key,
    w_value,
    w_output,
    w_gate,
    w_up,
    w_down,
    norm_attn,
    norm_ffn,
    norm_query,
    norm_key,
    cotangent,
):
    rows_own, q_width = w_query.shape
    kv_width = w_key.shape[1]
    ff_width = w_gate.shape[1]
    row_count, width = tokens.shape
    half = width // 2
    head_size = 64
    gain_block = jnp.concatenate(
        [
            norm_attn[:, None],
            norm_ffn[:, None],
            jnp.broadcast_to(norm_query[:, None], (rows_own, 1)),
            jnp.broadcast_to(norm_key[:, None], (rows_own, 1)),
            jnp.zeros((rows_own, 124), bf16),
        ],
        axis=1,
    )
    attn = [
        Gather(jnp.concatenate([w_query, w_key], axis=1), ORDERS[0]),
        Gather(jnp.concatenate([w_value, w_output.T, gain_block], axis=1), ORDERS[2]),
    ]
    ffn = [
        Gather(w_gate, ORDERS[1]),
        Gather(w_up, ORDERS[3]),
        Gather(w_down.T, ORDERS[2]),
    ]
    for step in range(len(INNER)):
        ahead = [g.held for g in attn]
        gots = exchange(ahead, [g.bit for g in attn])
        late = exchange([g.held for g in ffn], [g.bit for g in ffn], ahead)
        for g, got in zip(attn, gots):
            g.take(got)
        for g, got in zip(ffn, late):
            g.take(got)
    mine = [g.rows() for g in attn]
    theirs = exchange(mine, ["c", "c"])
    w_qk = jnp.concatenate([mine[0], theirs[0]], axis=0)
    w_vog = jnp.concatenate([mine[1], theirs[1]], axis=0)
    mine = [g.rows() for g in ffn]
    theirs = exchange(mine, ["c", "c", "c"])
    gate_own, up_own, down_own = mine
    gate_other, up_other, down_other = theirs

    absolute = absolute_rows(width)
    relative = (
        lax.broadcasted_iota(jnp.int32, (width, width), 0) == absolute
    ).astype(bf16)
    head_rows = (
        lax.broadcasted_iota(jnp.int32, (head_size, width), 0) * rows_own == absolute
    ).astype(bf16)
    tokens = matmul(tokens, relative).astype(bf16)
    cotangent = matmul(cotangent, relative).astype(bf16)
    cot_own, cot_other = cotangent[:, :half], cotangent[:, half:]

    gains = w_vog[:, kv_width + q_width :].T
    gain_heads = matmul_tr(gains[:8], head_rows)
    gains = gains[:8].astype(f32)
    gain_attn, gain_ffn = gains[0], gains[1]
    gain_query, gain_key = gain_heads[2], gain_heads[3]
    w_v = w_vog[:, :kv_width]
    w_o = w_vog[:, kv_width : kv_width + q_width]

    head_count = q_width // head_size
    kv_count = kv_width // head_size
    allowed, cos_table, sin_table = tables(segment, head_size)
    inputs = tokens.astype(f32)
    normed_one, inv_one = normalize(inputs)
    hidden_one = (normed_one * gain_attn).astype(bf16)
    qk_raw = matmul(hidden_one, w_qk)
    query_raw = qk_raw[:, :q_width].reshape(row_count, head_count, head_size)
    key_raw = qk_raw[:, q_width:].reshape(row_count, kv_count, head_size)
    value_heads = matmul(hidden_one, w_v).astype(bf16).reshape(row_count, kv_count, head_size)
    query_rot, query_unit, query_inv = head_prep(query_raw, gain_query, cos_table, sin_table)
    key_rot, key_unit, key_inv = head_prep(key_raw, gain_key, cos_table, sin_table)
    query_heads = query_rot.astype(bf16)
    key_heads = key_rot.astype(bf16)
    attended, log_total = attend(query_heads, key_heads, value_heads, allowed)
    low = matmul_tr(attended, w_o).astype(bf16)
    residual = inputs + add_pair(low, swap_pair(low))
    normed_two, inv_two = normalize(residual)
    hidden_two = (normed_two * gain_ffn).astype(bf16)
    hid_own, hid_other = hidden_two[:, :half], hidden_two[:, half:]
    gate_pre = matmul(hid_own, gate_own) + matmul(hid_other, gate_other)
    up_pre = matmul(hid_own, up_own) + matmul(hid_other, up_other)
    sigmoid_gate = jax.nn.sigmoid(gate_pre)
    activation = (gate_pre * sigmoid_gate * up_pre).astype(bf16)
    grad_act = matmul(cot_own, down_own) + matmul(cot_other, down_other)
    grad_gate_pre = (
        grad_act * up_pre * sigmoid_gate * (1.0 + gate_pre * (1.0 - sigmoid_gate))
    ).astype(bf16)
    grad_up_pre = (grad_act * gate_pre * sigmoid_gate).astype(bf16)

    low = jnp.concatenate(
        [
            matmul_tr(grad_gate_pre, gate_own) + matmul_tr(grad_up_pre, up_own),
            matmul_tr(grad_gate_pre, gate_other) + matmul_tr(grad_up_pre, up_other),
        ],
        axis=1,
    ).astype(bf16)
    other = swap_pair(low)
    third = 2 * ff_width // 3
    grad_pre = jnp.concatenate([grad_gate_pre, grad_up_pre], axis=1)
    rights = [grad_pre[:, i * third : (i + 1) * third] for i in range(3)] + [activation]
    out_left = [hid_other] * 3 + [cot_other]
    own_left = [hid_own] * 3 + [cot_own]
    fed = [Reduce(ORDERS[i]) for i in (1, 2, 3, 0)]
    gots = exchange(
        [tr_matmul(a, b).astype(bf16) for a, b in zip(out_left, rights)], ["c"] * 4, [low]
    )
    for stream, a, b, got in zip(fed, own_left, rights, gots):
        stream.begin(tr_matmul(a, b), got)
    (low, other) = tie(fed, [low, other])

    advance(fed)
    grad_hidden_two = add_pair(low, other)
    grad_norm_ffn = jnp.sum(grad_hidden_two * normed_two, axis=0)
    grad_residual = cotangent.astype(f32) + norm_back(
        grad_hidden_two * gain_ffn, normed_two, inv_two
    )
    grad_res_low = grad_residual.astype(bf16)
    grad_attended = matmul(grad_res_low, w_o).astype(bf16)
    grads = attend_back(
        query_heads, key_heads, value_heads, attended, grad_attended, log_total, allowed
    )
    grads = tie(fed, list(grads) + [activation])
    activation = grads.pop()

    advance(fed)
    grad_q_rot, grad_k_rot, grad_kv_value = grads
    grad_q_raw, part_norm_query = head_back(
        grad_q_rot, query_unit, query_inv, gain_query, cos_table, sin_table
    )
    grad_k_raw, part_norm_key = head_back(
        grad_k_rot, key_unit, key_inv, gain_key, cos_table, sin_table
    )
    query_low = grad_q_raw.reshape(row_count, head_count * head_size).astype(bf16)
    key_low = grad_k_raw.reshape(row_count, kv_count * head_size).astype(bf16)
    value_low = grad_kv_value.reshape(row_count, kv_count * head_size).astype(bf16)
    low_out = jnp.concatenate(
        [matmul_tr(activation, down_own), matmul_tr(activation, down_other)], axis=1
    ).astype(bf16)
    query_low, key_low, value_low, low_out = tie(fed, [query_low, key_low, value_low, low_out])

    advance(fed)
    partial_one = matmul_tr(jnp.concatenate([query_low, key_low], axis=1), w_qk) + matmul_tr(
        value_low, w_v
    )
    low = partial_one.astype(bf16)
    other = swap_pair(low)
    other_out = swap_pair(low_out)
    head_gains = jnp.stack([part_norm_query, part_norm_key]).astype(bf16)
    gain_rows = jnp.concatenate(
        [
            jnp.sum(partial_one * normed_one, axis=0)[None],
            0.5 * grad_norm_ffn[None],
            matmul(head_gains, head_rows),
            jnp.zeros((124, width), f32),
        ],
        axis=0,
    ).astype(bf16)
    eye = (
        lax.broadcasted_iota(jnp.int32, (128, 128), 0)
        == lax.broadcasted_iota(jnp.int32, (128, 128), 1)
    ).astype(bf16)
    kv_low = jnp.concatenate([key_low, value_low], axis=1)

    def late_parts(at):
        side = slice(at * half, (at + 1) * half)
        return [
            jnp.concatenate(
                [tr_matmul(hidden_one[:, side], query_low), tr_matmul(gain_rows[:, side], eye)],
                axis=1,
            ),
            tr_matmul(hidden_one[:, side], kv_low),
            tr_matmul(grad_res_low[:, side], attended),
        ]

    late = [Reduce(ORDERS[i]) for i in (0, 2, 1)]
    gots = exchange([p.astype(bf16) for p in late_parts(1)], ["c"] * 3)
    for stream, own, got in zip(late, late_parts(0), gots):
        stream.begin(own, got)
    low, other, low_out, other_out = tie(fed + late, [low, other, low_out, other_out])

    advance(fed + late)
    grad_hidden_one = add_pair(low, other)
    grad_tokens = (
        grad_residual + norm_back(grad_hidden_one * gain_attn, normed_one, inv_one)
    ).astype(bf16)
    grad_tokens = matmul_tr(grad_tokens, relative).astype(bf16)
    block_out = (residual + add_pair(low_out, other_out)).astype(bf16)
    block_out = matmul_tr(block_out, relative).astype(bf16)
    advance(late + fed)
    advance(late)
    advance(late)
    advance(late)
    owned_gain = late[0].held[:, q_width:]
    owned_gain = owned_gain + swap_pair(owned_gain)
    owned_gu = jnp.concatenate([s.held for s in fed[:3]], axis=1)
    return (
        block_out,
        grad_tokens,
        late[0].held[:, :q_width],
        late[1].held[:, :kv_width],
        late[1].held[:, kv_width:],
        late[2].held.T,
        owned_gu[:, :ff_width],
        owned_gu[:, ff_width:],
        fed[3].held.T,
        owned_gain[:, 0],
        owned_gain[:, 1],
        owned_gain[:1, 2],
        owned_gain[:1, 3],
    )


def solution(mesh):
    fine = Mesh(mesh.devices.reshape(4, 2, 4, 2, 2), ("z", "h", "y", "c", "t"))
    weight = P(FSDP, "t")
    weight_tr = P("t", FSDP)
    rows = P(FSDP, None)
    vector = P(FSDP)
    return jax.shard_map(
        on_device,
        mesh=fine,
        in_specs=(
            rows,
            vector,
            weight,
            weight,
            weight,
            weight_tr,
            weight,
            weight,
            weight_tr,
            vector,
            vector,
            vector,
            vector,
            rows,
        ),
        out_specs=(
            rows,
            rows,
            weight,
            weight,
            weight,
            weight_tr,
            weight,
            weight,
            weight_tr,
            vector,
            vector,
            vector,
            vector,
        ),
        check_vma=False,
    )
```

```python
import jax
import jax.numpy as jnp
from jax import lax
from jax.experimental import pallas as pl
from jax.experimental.pallas import tpu as pltpu
from jax.sharding import Mesh
from jax.sharding import PartitionSpec as P

epsilon = 1e-05
rope_base = 1000000.0
bf16 = jnp.bfloat16
f32 = jnp.float32
FSDP = ("z", "h", "y", "c")
BITS = {
    "c": ("c", 2, 1),
    "ya": ("y", 4, 1),
    "yb": ("y", 4, 3),
    "za": ("z", 4, 1),
    "zb": ("z", 4, 3),
    "h": ("h", 2, 1),
}


def matmul(matrix, second):
    return jnp.dot(matrix, second, preferred_element_type=f32)


def matmul_tr(matrix, second):
    return lax.dot_general(matrix, second, (((1,), (1,)), ((), ())), preferred_element_type=f32)


def tr_matmul(matrix, second):
    return lax.dot_general(matrix, second, (((0,), (0,)), ((), ())), preferred_element_type=f32)


def normalize(vector):
    inverse = lax.rsqrt(jnp.mean(vector * vector, axis=-1, keepdims=True) + epsilon)
    return (vector * inverse, inverse)


def norm_back(grad_in, normed, inverse):
    return inverse * (grad_in - normed * jnp.mean(grad_in * normed, axis=-1, keepdims=True))


def tables(segment):
    row_count = segment.shape[0]
    row_index = jnp.arange(row_count, dtype=jnp.int32)
    same_segment = segment[:, None] == segment[None, :]
    first_row = jnp.min(jnp.where(same_segment, row_index[None, :], row_count), axis=1)
    position = (row_index - first_row).astype(f32)
    allowed = same_segment & (row_index[None, :] <= row_index[:, None])
    frequency = jnp.power(rope_base, -2.0 * jnp.arange(32, dtype=f32) / 64)
    phase_angle = position[:, None] * frequency[None, :]
    phase_angle = jnp.concatenate([phase_angle] * 4, axis=1)
    bias = jnp.where(allowed, 0.0, -1e30).astype(f32)
    return (jnp.cos(phase_angle), jnp.sin(phase_angle), bias)


def lanes(rows):
    return lax.broadcasted_iota(jnp.int32, (rows, 128), 1)


def turn(array, low_half, sign_low):
    up = pltpu.roll(array, 96, 1)
    down = pltpu.roll(array, 32, 1)
    return jnp.where(low_half, sign_low * up, -sign_low * down)


def head_mean(array, spread):
    high = array.astype(bf16)
    rest = (array - high.astype(f32)).astype(bf16)
    return matmul(high, spread) + matmul(rest, spread)


def spread_matrix():
    rows = lax.broadcasted_iota(jnp.int32, (128, 128), 0)
    return jnp.where(rows // 64 == lanes(128) // 64, 1.0 / 64, 0.0).astype(bf16)


def both_rows(pair):
    low = lanes(pair.shape[0]) < 64
    zero = jnp.zeros_like(pair)
    return jnp.concatenate([jnp.where(low, pair, zero), jnp.where(low, zero, pair)], axis=0)


def both_lanes(pair, odd):
    pair = pair.astype(f32)
    low = lanes(pair.shape[0]) < 64
    other = pltpu.roll(pair, 64, 1)
    picked = jnp.where(low, other, pair) if odd else jnp.where(low, pair, other)
    return picked.astype(bf16)


def side_by_side(stacked):
    rows = stacked.shape[0] // 2
    return jnp.where(lanes(rows) < 64, stacked[:rows], stacked[rows:])


def group(index):
    return slice(128 * index, 128 * index + 128)


def forward_kernel(
    normed_ref,
    w_qk_ref,
    w_vog_ref,
    head_rows_ref,
    cos_ref,
    sin_ref,
    bias_ref,
    hidden_ref,
    gains_ref,
    gain_heads_ref,
    raw_ref,
    rot_ref,
    value_ref,
    attended_ref,
    log_ref,
    low_ref,
):
    qk_width = w_qk_ref.shape[1]
    kv_width = qk_width // 3
    q_width = 2 * kv_width
    ends = kv_width + q_width
    pick = (
        lax.broadcasted_iota(jnp.int32, (8, 128), 0) == lax.broadcasted_iota(jnp.int32, (8, 128), 1)
    ).astype(bf16)
    gains = matmul_tr(pick, w_vog_ref[:, ends : ends + 128])
    gains_ref[...] = gains
    gain_heads = matmul_tr(gains.astype(bf16), head_rows_ref[...])
    gain_heads_ref[...] = gain_heads
    hidden = (normed_ref[...] * gains[0:1, :]).astype(bf16)
    hidden_ref[...] = hidden
    raw = matmul(hidden, w_qk_ref[...])
    raw_ref[...] = raw
    value = matmul(hidden, w_vog_ref[:, :kv_width]).astype(bf16)
    value_ref[...] = value
    rows = raw.shape[0]
    spread = spread_matrix()
    low_half = (lanes(rows) % 64) < 32
    cos, sin = cos_ref[...], sin_ref[...]
    turned = []
    for g in range(qk_width // 128):
        part = raw[:, group(g)]
        inverse = lax.rsqrt(head_mean(part * part, spread) + epsilon)
        row = 2 if 128 * g < q_width else 3
        scaled = part * inverse * gain_heads[row : row + 1, group(g)]
        rotated = (scaled * cos + turn(scaled, low_half, -1.0) * sin).astype(bf16)
        rot_ref[:, group(g)] = rotated
        turned.append(rotated)
    bias = jnp.concatenate([bias_ref[...], bias_ref[...]], axis=0)
    log_all = jnp.zeros((2 * rows, 128), f32)
    mixed = []
    for g in range(q_width // 128):
        key = both_lanes(turned[q_width // 128 + g // 2], g % 2)
        val = both_lanes(value[:, group(g // 2)], g % 2)
        scores = matmul_tr(both_rows(turned[g]), key) * 0.125 + bias
        row_max = jnp.max(scores, axis=-1, keepdims=True)
        exps = jnp.exp(scores - row_max)
        total = jnp.sum(exps, axis=-1, keepdims=True)
        weights = (exps / total).astype(bf16)
        log_all = jnp.where(lanes(2 * rows) == g, row_max + jnp.log(total), log_all)
        out = side_by_side(matmul(weights, val)).astype(bf16)
        attended_ref[:, group(g)] = out
        mixed.append(out)
    log_ref[...] = log_all
    low_ref[...] = matmul_tr(
        jnp.concatenate(mixed, axis=1), w_vog_ref[:, kv_width:ends]
    ).astype(bf16)


def backward_kernel(
    low_ref,
    other_ref,
    cot_ref,
    normed_two_ref,
    inv_two_ref,
    gains_ref,
    gain_heads_ref,
    normed_one_ref,
    raw_ref,
    rot_ref,
    value_ref,
    attended_ref,
    log_ref,
    cos_ref,
    sin_ref,
    bias_ref,
    w_qk_ref,
    w_vog_ref,
    head_rows_ref,
    grad_res_ref,
    res_low_ref,
    qk_low_ref,
    value_low_ref,
    low_one_ref,
    gain_rows_ref,
):
    qk_width = w_qk_ref.shape[1]
    kv_width = qk_width // 3
    q_width = 2 * kv_width
    ends = kv_width + q_width
    rows = low_ref.shape[0]
    grad_hidden = low_ref[...].astype(f32) + other_ref[...].astype(f32)
    normed_two = normed_two_ref[...]
    gain_rows_ref[...] = jnp.zeros_like(gain_rows_ref)
    gain_rows_ref[1:2, :] = 0.5 * jnp.sum(grad_hidden * normed_two, axis=0, keepdims=True)
    scaled = grad_hidden * gains_ref[1:2, :]
    grad_res = cot_ref[...].astype(f32) + norm_back(scaled, normed_two, inv_two_ref[...])
    grad_res_ref[...] = grad_res
    res_low = grad_res.astype(bf16)
    res_low_ref[...] = res_low
    grad_att = matmul(res_low, w_vog_ref[:, kv_width:ends]).astype(bf16)
    spread = spread_matrix()
    low_half = (lanes(rows) % 64) < 32
    cos, sin = cos_ref[...], sin_ref[...]
    bias = jnp.concatenate([bias_ref[...], bias_ref[...]], axis=0)
    grads = [None] * (qk_width // 128)
    halves_k, halves_v = [], []
    for g in range(q_width // 128):
        key = both_lanes(rot_ref[:, group(q_width // 128 + g // 2)], g % 2)
        val = both_lanes(value_ref[:, group(g // 2)], g % 2)
        query = both_rows(rot_ref[:, group(g)])
        scores = matmul_tr(query, key) * 0.125 + bias
        log_total = jnp.sum(
            jnp.where(lanes(2 * rows) == g, log_ref[...], 0.0), axis=-1, keepdims=True
        )
        prob = jnp.exp(scores - log_total)
        grad_two = both_rows(grad_att[:, group(g)])
        out_pair = attended_ref[:, group(g)].astype(f32)
        out_two = jnp.concatenate([out_pair, out_pair], axis=0)
        delta = jnp.sum(grad_two.astype(f32) * out_two, axis=-1, keepdims=True)
        grad_prob = matmul_tr(grad_two, val)
        grad_scores = (prob * (grad_prob - delta) * 0.125).astype(bf16)
        grads[g] = side_by_side(matmul(grad_scores, key))
        grad_k = tr_matmul(grad_scores, query)
        halves_k.append(grad_k + pltpu.roll(grad_k, 64, 1))
        grad_v = tr_matmul(prob.astype(bf16), grad_two)
        halves_v.append(grad_v + pltpu.roll(grad_v, 64, 1))
    first = lanes(rows) < 64
    value_parts = []
    for m in range(kv_width // 128):
        grads[q_width // 128 + m] = jnp.where(first, halves_k[2 * m], halves_k[2 * m + 1])
        part = jnp.where(first, halves_v[2 * m], halves_v[2 * m + 1]).astype(bf16)
        value_low_ref[:, group(m)] = part
        value_parts.append(part)
    lowered = []
    head_sums = []
    for g, grad in enumerate(grads):
        part = raw_ref[:, group(g)]
        inverse = lax.rsqrt(head_mean(part * part, spread) + epsilon)
        unit = part * inverse
        grad_scaled = grad * cos + turn(grad * sin, low_half, 1.0)
        head_sums.append(jnp.sum(grad_scaled * unit, axis=0, keepdims=True))
        row = 2 if 128 * g < q_width else 3
        grad_unit = grad_scaled * gain_heads_ref[row : row + 1, group(g)]
        back = inverse * (grad_unit - unit * head_mean(grad_unit * unit, spread))
        back = back.astype(bf16)
        qk_low_ref[:, group(g)] = back
        lowered.append(back)
    sums = jnp.concatenate(head_sums, axis=1)
    at = lax.broadcasted_iota(jnp.int32, (8, qk_width), 1)
    row_at = lax.broadcasted_iota(jnp.int32, (8, qk_width), 0)
    wanted = jnp.where(at < q_width, 0, 1)
    two = jnp.where(row_at == wanted, sums, 0.0).astype(bf16)
    placed = matmul(two, head_rows_ref[...])
    gain_rows_ref[2:4, :] = placed[0:2, :]
    partial = matmul_tr(jnp.concatenate(lowered, axis=1), w_qk_ref[...]) + matmul_tr(
        jnp.concatenate(value_parts, axis=1), w_vog_ref[:, :kv_width]
    )
    low_one_ref[...] = partial.astype(bf16)
    gain_rows_ref[0:1, :] = jnp.sum(partial * normed_one_ref[...], axis=0, keepdims=True)


def whole_call(kernel, shapes, *operands):
    return pl.pallas_call(
        kernel,
        out_shape=[jax.ShapeDtypeStruct(s, d) for s, d in shapes],
        in_specs=[pl.BlockSpec(memory_space=pltpu.VMEM)] * len(operands),
        out_specs=[pl.BlockSpec(memory_space=pltpu.VMEM)] * len(shapes),
        compiler_params=pltpu.CompilerParams(vmem_limit_bytes=40 * 2**20),
        cost_estimate=pl.CostEstimate(flops=1, bytes_accessed=1, transcendentals=0),
    )(*operands)


def swap(array, bit):
    axis, size, flip = BITS[bit]
    return lax.ppermute(array, axis, [(i, i ^ flip) for i in range(size)])


def swap_pair(low):
    return lax.ppermute(low, "t", [(0, 1), (1, 0)])


def add_pair(low, other):
    return low.astype(f32) + other.astype(f32)


def absolute_rows(width):
    block = width // 64
    r = lax.broadcasted_iota(jnp.int32, (1, width), 1)
    k = r % block
    bits = r // block
    h, zb, za, yb, ya, c = ((bits >> i) & 1 for i in range(6))
    z_at = lax.axis_index("z") ^ za ^ (3 * zb)
    y_at = lax.axis_index("y") ^ ya ^ (3 * yb)
    h_at = lax.axis_index("h") ^ h
    c_at = lax.axis_index("c") ^ c
    return (((z_at * 2 + h_at) * 4 + y_at) * 2 + c_at) * block + k


ORDERS = (
    ("ya", "yb", "za", "zb", "h"),
    ("yb", "ya", "zb", "za", "h"),
    ("za", "zb", "ya", "yb", "h"),
    ("zb", "za", "yb", "ya", "h"),
)
INNER = ("ya", "yb", "za", "zb", "h")


def exchange(arrays, bits, after=()):
    arrays = lax.optimization_barrier(tuple(arrays) + tuple(after))[: len(arrays)]
    return [swap(a.reshape(-1, a.shape[-1]), b).reshape(a.shape) for a, b in zip(arrays, bits)]


def join(first, second):
    both = lax.optimization_barrier(tuple(first) + tuple(second))
    return list(both[: len(first)]), list(both[len(first) :])


class Gather:
    def __init__(self, held, order, names=()):
        self.held = held
        self.order = list(order)
        self.names = list(names)

    @property
    def bit(self):
        return self.order[0]

    def take(self, got):
        bit = self.order.pop(0)
        self.names = [n for n in INNER if n in self.names or n == bit]
        self.held = jnp.stack([self.held, got], axis=self.names.index(bit))

    def split(self, widths, orders):
        parts, at = [], 0
        for extent, order in zip(widths, orders):
            parts.append(Gather(self.held[..., at : at + extent], order, self.names))
            at += extent
        return parts

    def rows(self):
        return self.held.reshape(-1, self.held.shape[-1])


class Reduce:
    def __init__(self, order):
        self.order = list(order)
        self.names = list(INNER)

    def begin(self, own, got):
        held = (own + got.astype(f32)).astype(bf16)
        rows = held.shape[0] // 2 ** len(self.names)
        self.held = held.reshape((2,) * len(self.names) + (rows, held.shape[1]))

    @property
    def bit(self):
        return self.order[0]

    def give(self):
        return lax.index_in_dim(self.held, 1, self.names.index(self.bit), keepdims=False)

    def take(self, got):
        own = lax.index_in_dim(self.held, 0, self.names.index(self.bit), keepdims=False)
        self.names.remove(self.order.pop(0))
        self.held = own.astype(f32) + got.astype(f32)
        if self.names:
            self.held = self.held.astype(bf16)


def merge(streams, order):
    whole = Reduce(order)
    whole.names = list(streams[0].names)
    whole.held = jnp.concatenate([s.held for s in streams], axis=-1)
    return whole


def advance(streams, after=()):
    gots = exchange([s.give() for s in streams], [s.bit for s in streams], after)
    for stream, got in zip(streams, gots):
        stream.take(got)


def tie(streams, values):
    held, values = join([s.held for s in streams], values)
    for stream, array in zip(streams, held):
        stream.held = array
    return values


def on_device(
    tokens,
    segment,
    w_query,
    w_key,
    w_value,
    w_output,
    w_gate,
    w_up,
    w_down,
    norm_attn,
    norm_ffn,
    norm_query,
    norm_key,
    cotangent,
):
    rows_own, q_width = w_query.shape
    kv_width = w_key.shape[1]
    ff_width = w_gate.shape[1]
    row_count, width = tokens.shape
    half = width // 2
    head_size = 64
    gain_block = jnp.concatenate(
        [
            norm_attn[:, None],
            norm_ffn[:, None],
            jnp.broadcast_to(norm_query[:, None], (rows_own, 1)),
            jnp.broadcast_to(norm_key[:, None], (rows_own, 1)),
            jnp.zeros((rows_own, 124), bf16),
        ],
        axis=1,
    )
    attn_all = Gather(
        jnp.concatenate([w_query, w_key, w_value, w_output.T, gain_block], axis=1), ("h", "zb")
    )
    ffn_all = Gather(jnp.concatenate([w_gate, w_up, w_down.T], axis=1), ("h",))

    def step(first, second):
        ahead = [g.held for g in first]
        gots = exchange(ahead, [g.bit for g in first])
        late = exchange([g.held for g in second], [g.bit for g in second], ahead)
        for g, got in zip(first + second, gots + late):
            g.take(got)

    step([attn_all], [ffn_all])
    ffn = ffn_all.split(
        (ff_width, ff_width, ff_width),
        (("za", "zb", "ya", "yb"), ("ya", "yb", "za", "zb"), ("yb", "ya", "zb", "za")),
    )
    step([attn_all], ffn)
    attn = attn_all.split(
        (q_width + kv_width, kv_width + q_width + 128), (("za", "yb", "ya"), ("yb", "ya", "za"))
    )
    step(attn, ffn)
    step(attn, ffn)
    ahead = [g.held for g in attn]
    gots = exchange(ahead, [g.bit for g in attn])
    ffn_last = exchange([g.held for g in ffn], [g.bit for g in ffn], ahead)
    for g, got in zip(attn, gots):
        g.take(got)
    mine = [g.rows() for g in attn]
    theirs = exchange(mine, ["c", "c"])
    w_qk = jnp.concatenate([mine[0], theirs[0]], axis=0)
    w_vog = jnp.concatenate([mine[1], theirs[1]], axis=0)

    absolute = absolute_rows(width)
    relative = (
        lax.broadcasted_iota(jnp.int32, (width, width), 0) == absolute
    ).astype(bf16)
    head_rows = (
        (lax.broadcasted_iota(jnp.int32, (q_width + kv_width, width), 0) % head_size) * rows_own
        == absolute
    ).astype(bf16)
    tokens = matmul(tokens, relative).astype(bf16)
    cotangent = matmul(cotangent, relative).astype(bf16)
    cot_own, cot_other = cotangent[:, :half], cotangent[:, half:]

    cos_table, sin_table, bias = tables(segment)
    inputs = tokens.astype(f32)
    normed_one, inv_one = normalize(inputs)
    qk_width = q_width + kv_width
    hidden_one, gains, gain_heads, qk_raw, qk_rot, value, attended, log_total, low = whole_call(
        forward_kernel,
        (
            ((row_count, width), bf16),
            ((8, width), f32),
            ((8, qk_width), f32),
            ((row_count, qk_width), f32),
            ((row_count, qk_width), bf16),
            ((row_count, kv_width), bf16),
            ((row_count, q_width), bf16),
            ((2 * row_count, 128), f32),
            ((row_count, width), bf16),
        ),
        normed_one,
        w_qk,
        w_vog,
        head_rows,
        cos_table,
        sin_table,
        bias,
    )
    gain_attn, gain_ffn = gains[0], gains[1]
    ffn_last, _ = join(ffn_last, [low])
    for g, got in zip(ffn, ffn_last):
        g.take(got)
    gate_own, up_own, down_own = [g.rows() for g in ffn]
    gate_other, up_other, down_other = exchange([gate_own, up_own, down_own], ["c"] * 3)
    residual = inputs + add_pair(low, swap_pair(low))
    normed_two, inv_two = normalize(residual)
    hidden_two = (normed_two * gain_ffn).astype(bf16)
    hid_own, hid_other = hidden_two[:, :half], hidden_two[:, half:]
    gate_pre = matmul(hid_own, gate_own) + matmul(hid_other, gate_other)
    up_pre = matmul(hid_own, up_own) + matmul(hid_other, up_other)
    sigmoid_gate = jax.nn.sigmoid(gate_pre)
    activation = (gate_pre * sigmoid_gate * up_pre).astype(bf16)
    grad_act = matmul(cot_own, down_own) + matmul(cot_other, down_other)
    grad_gate_pre = (
        grad_act * up_pre * sigmoid_gate * (1.0 + gate_pre * (1.0 - sigmoid_gate))
    ).astype(bf16)
    grad_up_pre = (grad_act * gate_pre * sigmoid_gate).astype(bf16)

    low = jnp.concatenate(
        [
            matmul_tr(grad_gate_pre, gate_own) + matmul_tr(grad_up_pre, up_own),
            matmul_tr(grad_gate_pre, gate_other) + matmul_tr(grad_up_pre, up_other),
        ],
        axis=1,
    ).astype(bf16)
    other = swap_pair(low)
    grad_pre = jnp.concatenate([grad_gate_pre, grad_up_pre], axis=1)
    (grad_pre, act), _ = join([grad_pre, activation], [low])
    cut = (1792, 3456, 1792)

    def ffn_parts(hid, cot):
        return [
            tr_matmul(hid, grad_pre[:, : cut[0]]),
            tr_matmul(hid, grad_pre[:, cut[0] : cut[1]]),
            jnp.concatenate(
                [tr_matmul(hid, grad_pre[:, cut[1] :]), tr_matmul(cot, act[:, cut[2] :])], axis=1
            ),
            tr_matmul(cot, act[:, : cut[2]]),
        ]

    fed = [Reduce(ORDERS[i]) for i in (1, 2, 3, 0)]
    gots = exchange([p.astype(bf16) for p in ffn_parts(hid_other, cot_other)], ["c"] * 4)
    for stream, own, got in zip(fed, ffn_parts(hid_own, cot_own), gots):
        stream.begin(own, got)
    low, other, activation = tie(fed, [low, other, activation])

    advance(fed)
    grad_residual, grad_res_low, qk_low, value_low, low, gain_rows = whole_call(
        backward_kernel,
        (
            ((row_count, width), f32),
            ((row_count, width), bf16),
            ((row_count, qk_width), bf16),
            ((row_count, kv_width), bf16),
            ((row_count, width), bf16),
            ((128, width), f32),
        ),
        low,
        other,
        cotangent,
        normed_two,
        inv_two,
        gains,
        gain_heads,
        normed_one,
        qk_raw,
        qk_rot,
        value,
        attended,
        log_total,
        cos_table,
        sin_table,
        bias,
        w_qk,
        w_vog,
        head_rows,
    )
    gain_rows = gain_rows[:8]
    gain_rows = (gain_rows + swap_pair(gain_rows)).astype(bf16)
    other = swap_pair(low)
    low_out = jnp.concatenate(
        [matmul_tr(activation, down_own), matmul_tr(activation, down_other)], axis=1
    ).astype(bf16)
    other_out = swap_pair(low_out)
    eye = (
        lax.broadcasted_iota(jnp.int32, (8, 128), 0)
        == lax.broadcasted_iota(jnp.int32, (8, 128), 1)
    ).astype(bf16)

    def late_parts(at):
        side = slice(at * half, (at + 1) * half)
        return [
            tr_matmul(hidden_one[:, side], qk_low),
            jnp.concatenate(
                [
                    tr_matmul(hidden_one[:, side], value_low),
                    tr_matmul(grad_res_low[:, side], attended),
                    tr_matmul(gain_rows[:, side], eye),
                ],
                axis=1,
            ),
        ]

    late = [Reduce(ORDERS[i][:2]) for i in (0, 1)]
    gots = exchange([p.astype(bf16) for p in late_parts(1)], ["c"] * 2)
    for stream, own, got in zip(late, late_parts(0), gots):
        stream.begin(own, got)
    low, other, low_out, other_out = tie(fed + late, [low, other, low_out, other_out])

    advance(late + fed)
    grad_hidden_one = add_pair(low, other)
    grad_tokens = (
        grad_residual + norm_back(grad_hidden_one * gain_attn, normed_one, inv_one)
    ).astype(bf16)
    grad_tokens = matmul_tr(grad_tokens, relative).astype(bf16)
    block_out = (residual + add_pair(low_out, other_out)).astype(bf16)
    block_out = matmul_tr(block_out, relative).astype(bf16)
    advance(late + fed)
    late = merge(late, ("za", "zb", "h"))
    advance([late] + fed)
    done = merge(fed, ("h",))
    advance([late, done])
    advance([late])
    late, done = late.held, done.held
    ends = (q_width, q_width + kv_width, q_width + 2 * kv_width, 2 * (q_width + kv_width))
    owned_gain = late[:, ends[3] :]
    down_at = 2 * ff_width
    owned_down = jnp.concatenate([done[:, down_at + 512 :], done[:, down_at : down_at + 512]], axis=1)
    return (
        block_out,
        grad_tokens,
        late[:, : ends[0]],
        late[:, ends[0] : ends[1]],
        late[:, ends[1] : ends[2]],
        late[:, ends[2] : ends[3]].T,
        done[:, :ff_width],
        done[:, ff_width:down_at],
        owned_down.T,
        owned_gain[:, 0],
        owned_gain[:, 1],
        owned_gain[:1, 2],
        owned_gain[:1, 3],
    )


def solution(mesh):
    fine = Mesh(mesh.devices.reshape(4, 2, 4, 2, 2), ("z", "h", "y", "c", "t"))
    weight = P(FSDP, "t")
    weight_tr = P("t", FSDP)
    rows = P(FSDP, None)
    vector = P(FSDP)
    return jax.shard_map(
        on_device,
        mesh=fine,
        in_specs=(
            rows,
            vector,
            weight,
            weight,
            weight,
            weight_tr,
            weight,
            weight,
            weight_tr,
            vector,
            vector,
            vector,
            vector,
            rows,
        ),
        out_specs=(
            rows,
            rows,
            weight,
            weight,
            weight,
            weight_tr,
            weight,
            weight,
            weight_tr,
            vector,
            vector,
            vector,
            vector,
        ),
        check_vma=False,
    )
```
